256 devices in a mesh: aux: 4 (over x_hi, core), row: 64 (over z, x_lo, y).
Axes of the slice: x: 4 (x_hi: 2, x_lo: 2; x = x_hi * 2 + x_lo), y: 4, z: 8, core: 2. Of those that a mesh axis runs over, the one named last changes fastest.
Arguments:
- integrals: bfloat16 [4, 8192, 8192], P('aux', 'row'), may hold values from -6 to 6
- orbitals: bfloat16 [8192, 768], P('row'), may hold values from -0.0011901855 to 0.0011901855
Outputs:
- exchange_matrix: float32 [8192, 8192], P('row', 'aux')
The draws below stay inside these ranges and needn't reach their ends.
All inputs are finite; a program needn't handle non-finite values.
Results may differ from the reference program's by a relative error of at most 0.0033.
Values may be sent and summed in bfloat16 or wider, within the bound.
No kernel may reach another device: no remote copies, remote signals or barrier semaphores. Data moves between devices by JAX's collectives and lax.ppermute only.
A program may use at most 128 MiB of HBM per device.

```python
import jax
import jax.numpy as jnp

N = 8192
OCC = 768
NAUX = 4


def levels(stream_key, shape, pieces, smallest, largest):
    gain = 1.0
    for position, parts in pieces:
        steps = jax.random.uniform(jax.random.fold_in(jax.random.fold_in(stream_key, 6), position), (parts,), jnp.float32, smallest / len(pieces), largest / len(pieces))
        gain = gain * jnp.repeat(jnp.exp(steps), shape[position] // parts).reshape((-1,) + (1,) * (len(shape) - 1 - position))
    return gain


def normal_values(rng, dims, spread, limit, cuts=(), dtype=jnp.bfloat16):
    values = spread * jax.random.normal(rng, dims, jnp.float32)
    if cuts:
        values = values * levels(rng, dims, cuts, -0.22, 0.18)
    return jnp.clip(values, -limit, limit).astype(dtype)


def setup_inputs(seed: int = 0) -> dict:
    arg_keys = jax.random.split(jax.random.key(seed), 3)
    return {
        "integrals": normal_values(arg_keys[0], (NAUX, N, N), 1.0, 6.0, ((0, 4), (1, 64))),
        "orbitals": normal_values(arg_keys[1], (N, OCC), ((N * NAUX * OCC) ** -0.5), 0.0011901855, ((0, 64),)),
    }


def reference(integrals, orbitals):
    halves = []
    for index in range(NAUX):
        product = jnp.dot(integrals[index], orbitals, preferred_element_type=jnp.float32)
        halves.append(product.astype(jnp.bfloat16))
    joined = jnp.concatenate(halves, axis=1)
    return jnp.dot(joined, joined.T, preferred_element_type=jnp.float32)
```

```python
import jax
import jax.numpy as jnp
from jax import lax
from jax.experimental import pallas as pl
from jax.experimental.pallas import tpu as pltpu
from jax.sharding import Mesh
from jax.sharding import PartitionSpec as P

AXES = ("x_hi", "core", "z", "x_lo", "y")
SIZES = (2, 2, 8, 2, 4)
NZ, NX, NY = 8, 2, 4
ROWS = 128
N = 8192
OCC = 768
COLS = OCC // 2
WIDTH = 128
F32 = jnp.float32
BF16 = jnp.bfloat16


def ring_pairs(size, step):
    pairs = []
    for core in range(2):
        sign = 1 - 2 * core
        for i in range(size):
            pairs.append((core * size + i, core * size + (i + sign * step) % size))
    return pairs


def ring_send(x, axis, step):
    size = SIZES[AXES.index(axis)]
    return lax.ppermute(x, ("core", axis), ring_pairs(size, step))


def x_send(x):
    pairs = []
    for core in range(2):
        for i in range(4):
            j = (i + 1 - 2 * core) % 4
            src = ((i // 2) * 2 + core) * 2 + i % 2
            dst = ((j // 2) * 2 + core) * 2 + j % 2
            pairs.append((src, dst))
    return lax.ppermute(x, ("x_hi", "core", "x_lo"), pairs)


def swap(x, axes, flips):
    sizes = [SIZES[AXES.index(a)] for a in axes]
    total = 1
    for s in sizes:
        total *= s
    mask = 0
    for f in flips:
        mask = mask * 2 + f
    return lax.ppermute(x, axes, [(i, i ^ mask) for i in range(total)])


RING = {"z": (0, -1, 1, -2, 2, -3, 3, -4), "y": (0, -1, 1, -2), "x": (0, 1)}


def ring_gather(x, axis):
    if axis == "x":
        return [x, x_send(x)]
    size = SIZES[AXES.index(axis)]
    fwd, bwd, out = x, x, [x]
    for k in range(1, size // 2 + 1):
        fwd = ring_send(fwd, axis, 1)
        out.append(fwd)
        if 2 * k < size:
            bwd = ring_send(bwd, axis, -1)
            out.append(bwd)
    return out


ORDERS = (("x", "y", "z"), ("z", "x", "y"), ("z", "y", "x"))


def gather_part(x, order):
    for axis in order[:-1]:
        x = jnp.concatenate(ring_gather(x, axis), axis=0)
    return ring_gather(x, order[-1])


def block_index(offsets):
    sign = 1 - 2 * lax.axis_index("core")
    z = (lax.axis_index("z") + sign * offsets["z"]) % NZ
    x = (lax.axis_index("x_lo") + offsets["x"]) % NX
    y = (lax.axis_index("y") + sign * offsets["y"]) % NY
    return (z * NX + x) * NY + y


def part_offsets(order):
    first, second, last = order
    return [
        {first: a, second: b, last: c}
        for c in RING[last]
        for b in RING[second]
        for a in RING[first]
    ]


def arrange_kernel(own_ref, sib_ref, *outs):
    for order, out in zip(ORDERS, outs):
        for j, offsets in enumerate(part_offsets(order)):
            start = pl.multiple_of(block_index(offsets) * ROWS, ROWS)
            out[:ROWS, j * ROWS : (j + 1) * ROWS] = own_ref[:, pl.ds(start, ROWS)]
            out[ROWS:, j * ROWS : (j + 1) * ROWS] = sib_ref[:, pl.ds(start, ROWS)]


def arrange(own, sib):
    shape = jax.ShapeDtypeStruct((2 * ROWS, N), BF16)
    return pl.pallas_call(
        arrange_kernel,
        out_shape=[shape] * len(ORDERS),
        compiler_params=pltpu.CompilerParams(vmem_limit_bytes=48 << 20),
    )(own, sib)


def tile_kernel(*refs):
    z_blocks, xy_blocks = refs[:8], refs[8:16]
    send_ref, keep_ref, z_buf, xy_buf, sems = refs[16:]
    core = lax.axis_index("core")
    sign = 1 - 2 * core
    z = lax.axis_index("z")
    copies = []
    for k, off in enumerate(RING["z"]):
        slot = (z + sign * off) % NZ
        copies.append(pltpu.make_async_copy(z_blocks[k], z_buf.at[slot], sems.at[k]))
    for k in range(8):
        copies.append(pltpu.make_async_copy(xy_blocks[k], xy_buf.at[k], sems.at[8 + k]))
    for c in copies:
        c.start()
    for c in copies:
        c.wait()
    for out, low in ((send_ref, 1 - core), (keep_ref, core)):
        for high in range(2):
            rhs = z_buf[pl.ds(4 * high + 2 * low, 2)].reshape(2 * ROWS, OCC)
            for k in range(8):
                out[high, k] = lax.dot_general(
                    xy_buf[k], rhs, (((1,), (1,)), ((), ())), preferred_element_type=F32
                ).astype(out.dtype)


def tile_product(z_blocks, xy_blocks):
    anyspace = pl.BlockSpec(memory_space=pl.ANY)
    shape = (2, 8, ROWS, 2 * ROWS)
    return pl.pallas_call(
        tile_kernel,
        in_specs=[anyspace] * 16,
        out_shape=[jax.ShapeDtypeStruct(shape, BF16), jax.ShapeDtypeStruct(shape, F32)],
        scratch_shapes=[
            pltpu.VMEM((8, ROWS, OCC), BF16),
            pltpu.VMEM((8, ROWS, OCC), BF16),
            pltpu.SemaphoreType.DMA((16,)),
        ],
        compiler_params=pltpu.CompilerParams(vmem_limit_bytes=48 << 20),
    )(*z_blocks, *xy_blocks)


Y_STEPS = (0, 1, 2, 3)


def final_kernel(own_ref, *refs):
    recv, out = refs[:-1], refs[-1]
    x_lo, y = lax.axis_index("x_lo"), lax.axis_index("y")
    for k, step in enumerate(Y_STEPS):
        src_y = (y - step) % NY
        for dx in range(2):
            src_x = (x_lo + dx) % NX
            for zl in range(2):
                start = pl.multiple_of(((zl * NX + src_x) * NY + src_y) * ROWS, ROWS)
                piece = slice(zl * ROWS, (zl + 1) * ROWS)
                val = own_ref[dx, :, piece] if k == 0 else recv[k - 1][dx, :, piece].astype(F32)
                out[:, pl.ds(start, ROWS)] = val


def assemble(own, received):
    return pl.pallas_call(
        final_kernel, out_shape=jax.ShapeDtypeStruct((ROWS, 16 * ROWS), F32)
    )(own, *received)


def body(integrals, orbitals):
    own = integrals[0]
    sib = swap(own, ("core",), (1,))
    core = lax.axis_index("core")
    mine = lax.dynamic_slice(orbitals, (0, core * COLS), (ROWS, COLS))
    parts = [mine[:, k * WIDTH : (k + 1) * WIDTH] for k in range(3)]
    gathered = [gather_part(part, order) for part, order in zip(parts, ORDERS)]
    arranged = arrange(own, sib)
    halves = []
    for blocks, lhs in zip(gathered, arranged):
        depth = N // len(blocks)
        total = None
        for k, block in enumerate(blocks):
            term = jnp.dot(lhs[:, k * depth : (k + 1) * depth], block, preferred_element_type=F32)
            total = term if total is None else total + term
        halves.append(total.astype(BF16))
    half = jnp.concatenate([h[:ROWS] for h in halves] + [h[ROWS:] for h in halves], axis=1)

    z_blocks = ring_gather(half, "z")
    pair = jnp.stack([half, swap(half, ("x_lo",), (1,))])
    lines = [pair] + [lax.ppermute(pair, "y", [(i, (i - s) % NY) for i in range(NY)]) for s in (1, 2, 3)]
    xy_blocks = [lines[s][dx] for dx in range(2) for s in range(4)]

    send, keep = tile_product(z_blocks, xy_blocks)
    total = keep + swap(send, ("core",), (1,)).astype(F32)
    total = total.reshape(2, 2, 4, ROWS, 2 * ROWS)
    a_hi = lax.axis_index("x_hi")
    near = lax.dynamic_index_in_dim(total, a_hi, 0, keepdims=False)
    far = lax.dynamic_index_in_dim(total, 1 - a_hi, 0, keepdims=False).astype(BF16)
    x_axes = ("x_hi", "x_lo")
    from_far = swap(far[0], x_axes, (1, 0))
    from_diag = swap(far[1], x_axes, (1, 1))
    from_near = swap(near[1].astype(BF16), x_axes, (0, 1))
    sums = jnp.stack([near[0] + from_far.astype(F32), from_near.astype(F32) + from_diag.astype(F32)])
    outgoing = sums[:, 1:].astype(BF16)
    received = [
        lax.ppermute(outgoing[:, s - 1], "y", [(i, (i + s) % NY) for i in range(NY)]) for s in (1, 2, 3)
    ]
    return assemble(sums[:, 0], received)


def solution(mesh):
    split = Mesh(mesh.devices.reshape(SIZES), AXES)
    row = ("z", "x_lo", "y")
    aux = ("x_hi", "core")
    return jax.shard_map(
        body,
        mesh=split,
        in_specs=(P(aux, row, None), P(row, None)),
        out_specs=P(row, aux),
        check_vma=False,
    )
```

```python
import jax
import jax.numpy as jnp
from jax import lax
from jax.experimental import pallas as pl
from jax.experimental.pallas import tpu as pltpu
from jax.sharding import Mesh
from jax.sharding import PartitionSpec as P

AXES = ("x_hi", "core", "z", "x_lo", "y")
SIZES = (2, 2, 8, 2, 4)
NZ, NX, NY = 8, 2, 4
ROWS = 128
N = 8192
OCC = 768
COLS = OCC // 2
WIDTH = 128
F32 = jnp.float32
BF16 = jnp.bfloat16


def ring_pairs(size, step):
    pairs = []
    for core in range(2):
        sign = 1 - 2 * core
        for i in range(size):
            pairs.append((core * size + i, core * size + (i + sign * step) % size))
    return pairs


def ring_send(x, axis, step):
    size = SIZES[AXES.index(axis)]
    return lax.ppermute(x, ("core", axis), ring_pairs(size, step))


def x_send(x):
    pairs = []
    for core in range(2):
        for i in range(4):
            j = (i + 1 - 2 * core) % 4
            src = ((i // 2) * 2 + core) * 2 + i % 2
            dst = ((j // 2) * 2 + core) * 2 + j % 2
            pairs.append((src, dst))
    return lax.ppermute(x, ("x_hi", "core", "x_lo"), pairs)


def swap(x, axes, flips):
    sizes = [SIZES[AXES.index(a)] for a in axes]
    total = 1
    for s in sizes:
        total *= s
    mask = 0
    for f in flips:
        mask = mask * 2 + f
    return lax.ppermute(x, axes, [(i, i ^ mask) for i in range(total)])


RING = {"z": (0, -1, 1, -2, 2, -3, 3, -4), "y": (0, -1, 1, -2), "x": (0, 1)}


def ring_gather(x, axis):
    if axis == "x":
        return [x, x_send(x)]
    size = SIZES[AXES.index(axis)]
    fwd, bwd, out = x, x, [x]
    for k in range(1, size // 2 + 1):
        fwd = ring_send(fwd, axis, 1)
        out.append(fwd)
        if 2 * k < size:
            bwd = ring_send(bwd, axis, -1)
            out.append(bwd)
    return out


def gathered_by_exchange(x, axes):
    size = 1
    for axis in axes:
        size *= SIZES[AXES.index(axis)]
    return lax.all_to_all(jnp.broadcast_to(x, (size, *x.shape)), axes, 0, 0, tiled=True)


def dot(lhs, rhs):
    return jnp.dot(lhs, rhs, preferred_element_type=F32)


def half_kernel(own_ref, sib_ref, *refs):
    by_z, by_y, by_x, out = refs[:8], refs[8:12], refs[12:14], refs[14]
    sign = 1 - 2 * lax.axis_index("core")
    z, x, y = lax.axis_index("z"), lax.axis_index("x_lo"), lax.axis_index("y")

    def strided(ref, x, y):
        start = (x * NY + y) * ROWS
        cols = [pl.multiple_of(k * NX * NY * ROWS + start, ROWS) for k in range(NZ)]
        return jnp.concatenate([ref[:, pl.ds(c, ROWS)] for c in cols], axis=1)

    depth = NZ * ROWS
    for p, ref in enumerate((own_ref, sib_ref)):
        total = jnp.zeros((ROWS, WIDTH), F32)
        for k, off in enumerate(RING["z"]):
            at = (z + sign * off) % NZ
            lhs = ref[:, pl.ds(pl.multiple_of(at * NX * NY * ROWS, ROWS), NX * NY * ROWS)]
            total += dot(lhs, by_z[k][...])
        out[:, (3 * p) * WIDTH : (3 * p + 1) * WIDTH] = total.astype(BF16)
        total = jnp.zeros((ROWS, WIDTH), F32)
        for k, off in enumerate(RING["y"]):
            for dx in range(NX):
                lhs = strided(ref, (x + dx) % NX, (y + sign * off) % NY)
                total += dot(lhs, by_y[k][dx * depth : (dx + 1) * depth])
        out[:, (3 * p + 1) * WIDTH : (3 * p + 2) * WIDTH] = total.astype(BF16)
        total = jnp.zeros((ROWS, WIDTH), F32)
        for dx in range(NX):
            for k, off in enumerate(RING["y"]):
                lhs = strided(ref, (x + dx) % NX, (y + sign * off) % NY)
                total += dot(lhs, by_x[dx][k * depth : (k + 1) * depth])
        out[:, (3 * p + 2) * WIDTH : (3 * p + 3) * WIDTH] = total.astype(BF16)


def half_blocks(own, sib, by_z, by_y, by_x):
    return pl.pallas_call(
        half_kernel,
        out_shape=jax.ShapeDtypeStruct((ROWS, OCC), BF16),
        compiler_params=pltpu.CompilerParams(vmem_limit_bytes=48 << 20),
    )(own, sib, *by_z, *by_y, *by_x)


def tile_kernel(*refs):
    z_blocks, xy_blocks = refs[:8], refs[8:16]
    send_ref, keep_ref, z_buf, xy_buf, sems = refs[16:]
    core = lax.axis_index("core")
    sign = 1 - 2 * core
    z = lax.axis_index("z")
    copies = []
    for k, off in enumerate(RING["z"]):
        slot = (z + sign * off) % NZ
        copies.append(pltpu.make_async_copy(z_blocks[k], z_buf.at[slot], sems.at[k]))
    for k in range(8):
        copies.append(pltpu.make_async_copy(xy_blocks[k], xy_buf.at[k], sems.at[8 + k]))
    for c in copies:
        c.start()
    for c in copies:
        c.wait()
    for out, low in ((send_ref, 1 - core), (keep_ref, core)):
        for high in range(2):
            rhs = z_buf[pl.ds(4 * high + 2 * low, 2)].reshape(2 * ROWS, OCC)
            for k in range(0, 8, 4):
                prod = lax.dot_general(
                    xy_buf[k : k + 4].reshape(4 * ROWS, OCC),
                    rhs,
                    (((1,), (1,)), ((), ())),
                    preferred_element_type=F32,
                )
                out[high, k : k + 4] = prod.astype(out.dtype).reshape(4, ROWS, 2 * ROWS)


def tile_product(z_blocks, xy_blocks):
    anyspace = pl.BlockSpec(memory_space=pl.ANY)
    shape = (2, 8, ROWS, 2 * ROWS)
    return pl.pallas_call(
        tile_kernel,
        in_specs=[anyspace] * 16,
        out_shape=[jax.ShapeDtypeStruct(shape, BF16), jax.ShapeDtypeStruct(shape, F32)],
        scratch_shapes=[
            pltpu.VMEM((8, ROWS, OCC), BF16),
            pltpu.VMEM((8, ROWS, OCC), BF16),
            pltpu.SemaphoreType.DMA((16,)),
        ],
        compiler_params=pltpu.CompilerParams(vmem_limit_bytes=48 << 20),
    )(*z_blocks, *xy_blocks)


Y_STEPS = (0, 1, 2, 3)


def final_kernel(own_ref, *refs):
    recv, out = refs[:-1], refs[-1]
    x_lo, y = lax.axis_index("x_lo"), lax.axis_index("y")
    for k, step in enumerate(Y_STEPS):
        src_y = (y - step) % NY
        for dx in range(2):
            src_x = (x_lo + dx) % NX
            for zl in range(2):
                start = pl.multiple_of(((zl * NX + src_x) * NY + src_y) * ROWS, ROWS)
                piece = slice(zl * ROWS, (zl + 1) * ROWS)
                val = own_ref[dx, :, piece] if k == 0 else recv[k - 1][dx, :, piece].astype(F32)
                out[:, pl.ds(start, ROWS)] = val


def assemble(own, received):
    return pl.pallas_call(
        final_kernel, out_shape=jax.ShapeDtypeStruct((ROWS, 16 * ROWS), F32)
    )(own, *received)


def body(integrals, orbitals):
    own = integrals[0]
    sib = swap(own, ("core",), (1,))
    core = lax.axis_index("core")
    mine = lax.dynamic_slice(orbitals, (0, core * COLS), (ROWS, COLS))
    lines = gathered_by_exchange(mine[:, WIDTH:], ("z",)).reshape(NZ * ROWS, 2 * WIDTH)
    plane = gathered_by_exchange(mine[:, :WIDTH], ("x_lo", "y")).reshape(NX * NY * ROWS, WIDTH)
    by_z = ring_gather(plane, "z")
    by_y = ring_gather(jnp.concatenate(ring_gather(lines[:, :WIDTH], "x"), axis=0), "y")
    by_x = ring_gather(jnp.concatenate(ring_gather(lines[:, WIDTH:], "y"), axis=0), "x")
    half = half_blocks(own, sib, by_z, by_y, by_x)

    z_blocks = ring_gather(half, "z")
    pair = jnp.stack([half, swap(half, ("x_lo",), (1,))])
    lines = [pair] + [lax.ppermute(pair, "y", [(i, (i - s) % NY) for i in range(NY)]) for s in (1, 2, 3)]
    xy_blocks = [lines[s][dx] for dx in range(2) for s in range(4)]

    send, keep = tile_product(z_blocks, xy_blocks)
    total = keep + swap(send, ("core",), (1,)).astype(F32)
    total = total.reshape(2, 2, 4, ROWS, 2 * ROWS)
    a_hi = lax.axis_index("x_hi")
    near = lax.dynamic_index_in_dim(total, a_hi, 0, keepdims=False)
    far = lax.dynamic_index_in_dim(total, 1 - a_hi, 0, keepdims=False).astype(BF16)
    x_axes = ("x_hi", "x_lo")
    from_far = swap(far[0], x_axes, (1, 0))
    from_diag = swap(far[1], x_axes, (1, 1))
    from_near = swap(near[1].astype(BF16), x_axes, (0, 1))
    sums = jnp.stack([near[0] + from_far.astype(F32), from_near.astype(F32) + from_diag.astype(F32)])
    outgoing = sums[:, 1:].astype(BF16)
    received = [
        lax.ppermute(outgoing[:, s - 1], "y", [(i, (i + s) % NY) for i in range(NY)]) for s in (1, 2, 3)
    ]
    return assemble(sums[:, 0], received)


def solution(mesh):
    split = Mesh(mesh.devices.reshape(SIZES), AXES)
    row = ("z", "x_lo", "y")
    aux = ("x_hi", "core")
    return jax.shard_map(
        body,
        mesh=split,
        in_specs=(P(aux, row, None), P(row, None)),
        out_specs=P(row, aux),
        check_vma=False,
    )
```

```python
import jax
import jax.numpy as jnp
from jax import lax
from jax.experimental import pallas as pl
from jax.experimental.pallas import tpu as pltpu
from jax.sharding import Mesh
from jax.sharding import PartitionSpec as P

AXES = ("x_hi", "core", "z", "x_lo", "y")
SIZES = (2, 2, 8, 2, 4)
NZ, NX, NY = 8, 2, 4
ROWS = 128
N = 8192
OCC = 768
COLS = OCC // 2
WIDTH = 128
F32 = jnp.float32
BF16 = jnp.bfloat16


def ring_pairs(size, step):
    pairs = []
    for core in range(2):
        sign = 1 - 2 * core
        for i in range(size):
            pairs.append((core * size + i, core * size + (i + sign * step) % size))
    return pairs


def ring_send(x, axis, step):
    size = SIZES[AXES.index(axis)]
    return lax.ppermute(x, ("core", axis), ring_pairs(size, step))


def x_send(x):
    pairs = []
    for core in range(2):
        for i in range(4):
            j = (i + 1 - 2 * core) % 4
            src = ((i // 2) * 2 + core) * 2 + i % 2
            dst = ((j // 2) * 2 + core) * 2 + j % 2
            pairs.append((src, dst))
    return lax.ppermute(x, ("x_hi", "core", "x_lo"), pairs)


def swap(x, axes, flips):
    sizes = [SIZES[AXES.index(a)] for a in axes]
    total = 1
    for s in sizes:
        total *= s
    mask = 0
    for f in flips:
        mask = mask * 2 + f
    return lax.ppermute(x, axes, [(i, i ^ mask) for i in range(total)])


RING = {"z": (0, -1, 1, -2, 2, -3, 3, -4), "y": (0, -1, 1, -2), "x": (0, 1)}


class Ring:
    def __init__(self, x, axis):
        self.axis, self.size = axis, SIZES[AXES.index(axis)]
        self.fwd, self.bwd, self.blocks, self.k = x, x, [x], 0

    def step(self, count=1):
        for _ in range(count):
            self.k += 1
            self.fwd = ring_send(self.fwd, self.axis, 1)
            self.blocks.append(self.fwd)
            if 2 * self.k < self.size:
                self.bwd = ring_send(self.bwd, self.axis, -1)
                self.blocks.append(self.bwd)
        return self

    def finish(self):
        return self.step(self.size // 2 - self.k).blocks

    def wait_for(self, *others):
        self.fwd, self.bwd, *others = lax.optimization_barrier((self.fwd, self.bwd, *others))
        return others


def ring_gather(x, axis):
    if axis == "x":
        return [x, x_send(x)]
    return Ring(x, axis).finish()


def gathered_by_exchange(x, axes):
    size = 1
    for axis in axes:
        size *= SIZES[AXES.index(axis)]
    return lax.all_to_all(jnp.broadcast_to(x, (size, *x.shape)), axes, 0, 0, tiled=True)


def dot(lhs, rhs):
    return jnp.dot(lhs, rhs, preferred_element_type=F32)


def half_kernel(own_ref, sib_ref, *refs):
    by_z, by_y, by_x, out = refs[:8], refs[8:12], refs[12:14], refs[14]
    sign = 1 - 2 * lax.axis_index("core")
    x, y = lax.axis_index("x_lo"), lax.axis_index("y")
    z_line = [(lax.axis_index("z") + sign * off) % NZ for off in RING["z"]]
    depth = NZ * ROWS

    def plane(ref, z):
        return ref[:, pl.ds(pl.multiple_of(z * NX * NY * ROWS, ROWS), NX * NY * ROWS)]

    def line(ref, dx, off):
        start = (((x + dx) % NX) * NY + (y + sign * off) % NY) * ROWS
        cols = [pl.multiple_of(z * NX * NY * ROWS + start, ROWS) for z in z_line]
        return jnp.concatenate([ref[:, pl.ds(c, ROWS)] for c in cols], axis=1)

    for p, ref in enumerate((own_ref, sib_ref)):
        totals = [jnp.zeros((ROWS, WIDTH), F32) for _ in range(3)]
        for k, z in enumerate(z_line):
            totals[0] += dot(plane(ref, z), by_z[k][...])
        for k, off in enumerate(RING["y"]):
            for dx in range(NX):
                lhs = line(ref, dx, off)
                totals[1] += dot(lhs, by_y[k][dx * depth : (dx + 1) * depth])
                totals[2] += dot(lhs, by_x[dx][k * depth : (k + 1) * depth])
        for k, total in enumerate(totals):
            out[:, (3 * p + k) * WIDTH : (3 * p + k + 1) * WIDTH] = total.astype(BF16)


def half_blocks(own, sib, by_z, by_y, by_x):
    return pl.pallas_call(
        half_kernel,
        out_shape=jax.ShapeDtypeStruct((ROWS, OCC), BF16),
        compiler_params=pltpu.CompilerParams(vmem_limit_bytes=48 << 20),
    )(own, sib, *by_z, *by_y, *by_x)


def tile_kernel(keep, *refs):
    z_blocks, xy_blocks, refs = refs[:8], refs[8:16], refs[16:]
    added = refs[0] if keep else None
    out, z_buf, xy_buf, z_sem, xy_sem = refs[-5:]
    core = lax.axis_index("core")
    low = core if keep else 1 - core
    sign = 1 - 2 * core
    z, x, y = lax.axis_index("z"), lax.axis_index("x_lo"), lax.axis_index("y")
    copies = [
        pltpu.make_async_copy(z_blocks[k], z_buf.at[(z + sign * off) % NZ], z_sem.at[k])
        for k, off in enumerate(RING["z"])
    ]
    for k in range(8):
        slot = ((x + k // 4) % NX) * NY + (y + k % 4) % NY
        copies.append(pltpu.make_async_copy(xy_blocks[k], xy_buf.at[slot], xy_sem.at[k]))
    for c in copies:
        c.start()
    for c in copies:
        c.wait()
    for high in range(2):
        rhs = z_buf[pl.ds(4 * high + 2 * low, 2)].reshape(2 * ROWS, OCC)
        for k in range(0, 8, 4):
            prod = lax.dot_general(
                xy_buf[k : k + 4].reshape(4 * ROWS, OCC),
                rhs,
                (((1,), (1,)), ((), ())),
                preferred_element_type=F32,
            ).reshape(4, ROWS, 2 * ROWS)
            rows = slice(8 * high + k, 8 * high + k + 4)
            if keep:
                prod = prod + added[rows].astype(F32)
            out[rows] = prod.astype(BF16)


def tile_product(z_blocks, xy_blocks, *added):
    anyspace = pl.BlockSpec(memory_space=pl.ANY)
    keep = bool(added)
    return pl.pallas_call(
        lambda *refs: tile_kernel(keep, *refs),
        in_specs=[anyspace] * 16 + [pl.BlockSpec(memory_space=pltpu.VMEM)] * len(added),
        out_shape=jax.ShapeDtypeStruct((16, ROWS, 2 * ROWS), BF16),
        scratch_shapes=[
            pltpu.VMEM((8, ROWS, OCC), BF16),
            pltpu.VMEM((8, ROWS, OCC), BF16),
            pltpu.SemaphoreType.DMA((8,)),
            pltpu.SemaphoreType.DMA((8,)),
        ],
        compiler_params=pltpu.CompilerParams(vmem_limit_bytes=48 << 20),
    )(*z_blocks, *xy_blocks, *added)


def final_kernel(pieces, out):
    for src in range(NX * NY):
        total = pieces[src].astype(F32) + pieces[NX * NY + src].astype(F32)
        for zl in range(2):
            start = (zl * NX * NY + src) * ROWS
            out[:, start : start + ROWS] = total[:, zl * ROWS : (zl + 1) * ROWS]


def assemble(pieces):
    return pl.pallas_call(
        final_kernel, out_shape=jax.ShapeDtypeStruct((ROWS, 16 * ROWS), F32)
    )(pieces)


def body(integrals, orbitals):
    own = integrals[0]
    sib = swap(own, ("core",), (1,))
    core = lax.axis_index("core")
    mine = lax.dynamic_slice(orbitals, (0, core * COLS), (ROWS, COLS))
    plane = gathered_by_exchange(mine[:, :WIDTH], ("x_lo", "y")).reshape(NX * NY * ROWS, WIDTH)
    line_ring = Ring(mine[:, WIDTH:], "z").step()
    (plane,) = line_ring.wait_for(plane)
    line_ring.step(2)
    plane_ring = Ring(plane, "z").step()
    plane_ring.fwd, plane_ring.bwd = line_ring.wait_for(plane_ring.fwd, plane_ring.bwd)
    lines = jnp.concatenate(line_ring.finish(), axis=0)
    by_z = plane_ring.finish()
    by_y = ring_gather(jnp.concatenate(ring_gather(lines[:, :WIDTH], "x"), axis=0), "y")
    by_x = ring_gather(jnp.concatenate(ring_gather(lines[:, WIDTH:], "y"), axis=0), "x")
    half = half_blocks(own, sib, by_z, by_y, by_x)

    z_blocks = ring_gather(half, "z")
    pair = jnp.stack([half, swap(half, ("x_lo",), (1,))])
    lines = [pair] + [lax.ppermute(pair, "y", [(i, (i - s) % NY) for i in range(NY)]) for s in (1, 2, 3)]
    xy_blocks = [lines[s][dx] for dx in range(2) for s in range(4)]

    other = tile_product(z_blocks, xy_blocks)
    mine = tile_product(z_blocks, xy_blocks, swap(other, ("core",), (1,)))
    pieces = lax.all_to_all(mine, ("x_hi", "x_lo", "y"), 0, 0, tiled=True)
    return assemble(pieces)


def solution(mesh):
    split = Mesh(mesh.devices.reshape(SIZES), AXES)
    row = ("z", "x_lo", "y")
    aux = ("x_hi", "core")
    return jax.shard_map(
        body,
        mesh=split,
        in_specs=(P(aux, row, None), P(row, None)),
        out_specs=P(row, aux),
        check_vma=False,
    )
```

```python
import jax
import jax.numpy as jnp
from jax import lax
from jax.experimental import pallas as pl
from jax.experimental.pallas import tpu as pltpu
from jax.sharding import Mesh
from jax.sharding import PartitionSpec as P

AXES = ("x_hi", "core", "z", "x_lo", "y")
SIZES = (2, 2, 8, 2, 4)
NZ, NX, NY = 8, 2, 4
ROWS = 128
N = 8192
OCC = 768
COLS = OCC // 2
F32 = jnp.float32
BF16 = jnp.bfloat16


def ring_pairs(size, step):
    pairs = []
    for core in range(2):
        sign = 1 - 2 * core
        for i in range(size):
            pairs.append((core * size + i, core * size + (i + sign * step) % size))
    return pairs


def ring_send(x, axis, step):
    size = SIZES[AXES.index(axis)]
    return lax.ppermute(x, ("core", axis), ring_pairs(size, step))


def x_send(x):
    pairs = []
    for core in range(2):
        for i in range(4):
            j = (i + 1 - 2 * core) % 4
            src = ((i // 2) * 2 + core) * 2 + i % 2
            dst = ((j // 2) * 2 + core) * 2 + j % 2
            pairs.append((src, dst))
    return lax.ppermute(x, ("x_hi", "core", "x_lo"), pairs)


def swap(x, axes, flips):
    sizes = [SIZES[AXES.index(a)] for a in axes]
    total = 1
    for s in sizes:
        total *= s
    mask = 0
    for f in flips:
        mask = mask * 2 + f
    return lax.ppermute(x, axes, [(i, i ^ mask) for i in range(total)])


RING = {"z": (0, -1, 1, -2, 2, -3, 3, -4), "y": (0, -1, 1, -2), "x": (0, 1)}


class Ring:
    def __init__(self, x, axis):
        self.axis, self.size = axis, SIZES[AXES.index(axis)]
        self.fwd, self.bwd, self.blocks, self.k = x, x, [x], 0

    def step(self, count=1):
        for _ in range(count):
            self.k += 1
            self.fwd = ring_send(self.fwd, self.axis, 1)
            self.blocks.append(self.fwd)
            if 2 * self.k < self.size:
                self.bwd = ring_send(self.bwd, self.axis, -1)
                self.blocks.append(self.bwd)
        return self

    def wait_for(self, *others):
        self.fwd, self.bwd, *others = lax.optimization_barrier((self.fwd, self.bwd, *others))
        return others

    def finish(self):
        return self.step(self.size // 2 - self.k).blocks


def ring_gather(x, axis):
    if axis == "x":
        return [x, x_send(x)]
    return Ring(x, axis).finish()


def by_y_kernel(x_ref, out_ref):
    for y in range(NY):
        for k in range(NZ * NX):
            out_ref[y, :, k * ROWS : (k + 1) * ROWS] = x_ref[:, (k * NY + y) * ROWS : (k * NY + y + 1) * ROWS]


def columns_by_y(x):
    return pl.pallas_call(
        by_y_kernel, out_shape=jax.ShapeDtypeStruct((NY, ROWS, N // NY), BF16)
    )(x)


def partial_kernel(own_ref, sib_ref, *refs):
    chunks, out, rhs, sems = refs[:8], refs[8], refs[9], refs[10]
    sign = 1 - 2 * lax.axis_index("core")
    z, x = lax.axis_index("z"), lax.axis_index("x_lo")
    copies = []
    for k, off in enumerate(RING["z"]):
        for dx in range(NX):
            slot = ((z + sign * off) % NZ) * NX + (x + dx) % NX
            dst = rhs.at[pl.ds(pl.multiple_of(slot * ROWS, ROWS), ROWS)]
            copies.append(pltpu.make_async_copy(chunks[k].at[pl.ds(dx * ROWS, ROWS)], dst, sems.at[2 * k + dx]))
    for c in copies:
        c.start()
    for c in copies:
        c.wait()
    for p, ref in enumerate((own_ref, sib_ref)):
        prod = jnp.dot(ref[...].reshape(NY * ROWS, N // NY), rhs[...], preferred_element_type=F32)
        out[:, :, p * COLS : (p + 1) * COLS] = prod.reshape(NY, ROWS, COLS)


def partial_half(own, sib, chunks):
    anyspace = pl.BlockSpec(memory_space=pl.ANY)
    vmem = pl.BlockSpec(memory_space=pltpu.VMEM)
    return pl.pallas_call(
        partial_kernel,
        in_specs=[vmem, vmem] + [anyspace] * 8,
        out_shape=jax.ShapeDtypeStruct((NY, ROWS, OCC), F32),
        scratch_shapes=[pltpu.VMEM((N // NY, COLS), BF16), pltpu.SemaphoreType.DMA((16,))],
        compiler_params=pltpu.CompilerParams(vmem_limit_bytes=48 << 20),
    )(own, sib, *chunks)


def tile_kernel(keep, *refs):
    z_blocks, xy_blocks, refs = refs[:8], refs[8:16], refs[16:]
    added = refs[0] if keep else None
    out, z_buf, xy_buf, z_sem, xy_sem = refs[-5:]
    core = lax.axis_index("core")
    low = core if keep else 1 - core
    sign = 1 - 2 * core
    z, x, y = lax.axis_index("z"), lax.axis_index("x_lo"), lax.axis_index("y")
    copies = [
        pltpu.make_async_copy(z_blocks[k], z_buf.at[(z + sign * off) % NZ], z_sem.at[k])
        for k, off in enumerate(RING["z"])
    ]
    for k in range(8):
        slot = ((x + k // 4) % NX) * NY + (y + k % 4) % NY
        copies.append(pltpu.make_async_copy(xy_blocks[k], xy_buf.at[slot], xy_sem.at[k]))
    for c in copies:
        c.start()
    for c in copies:
        c.wait()
    for high in range(2):
        rhs = z_buf[pl.ds(4 * high + 2 * low, 2)].reshape(2 * ROWS, OCC)
        for k in range(0, 8, 4):
            prod = lax.dot_general(
                xy_buf[k : k + 4].reshape(4 * ROWS, OCC),
                rhs,
                (((1,), (1,)), ((), ())),
                preferred_element_type=F32,
            ).reshape(4, ROWS, 2 * ROWS)
            rows = slice(8 * high + k, 8 * high + k + 4)
            if keep:
                prod = prod + added[rows].astype(F32)
            out[rows] = prod.astype(BF16)


def tile_product(z_blocks, xy_blocks, *added):
    anyspace = pl.BlockSpec(memory_space=pl.ANY)
    keep = bool(added)
    return pl.pallas_call(
        lambda *refs: tile_kernel(keep, *refs),
        in_specs=[anyspace] * 16 + [pl.BlockSpec(memory_space=pltpu.VMEM)] * len(added),
        out_shape=jax.ShapeDtypeStruct((16, ROWS, 2 * ROWS), BF16),
        scratch_shapes=[
            pltpu.VMEM((8, ROWS, OCC), BF16),
            pltpu.VMEM((8, ROWS, OCC), BF16),
            pltpu.SemaphoreType.DMA((8,)),
            pltpu.SemaphoreType.DMA((8,)),
        ],
        compiler_params=pltpu.CompilerParams(vmem_limit_bytes=48 << 20),
    )(*z_blocks, *xy_blocks, *added)


def final_kernel(pieces, out):
    for src in range(NX * NY):
        total = pieces[src].astype(F32) + pieces[NX * NY + src].astype(F32)
        for zl in range(2):
            start = (zl * NX * NY + src) * ROWS
            out[:, start : start + ROWS] = total[:, zl * ROWS : (zl + 1) * ROWS]


def assemble(pieces):
    return pl.pallas_call(
        final_kernel, out_shape=jax.ShapeDtypeStruct((ROWS, 16 * ROWS), F32)
    )(pieces)


def body(integrals, orbitals):
    own = lax.all_to_all(columns_by_y(integrals[0]), "y", 0, 0, tiled=True)
    core = lax.axis_index("core")
    mine = lax.dynamic_slice(orbitals, (0, core * COLS), (ROWS, COLS))
    ring = Ring(jnp.concatenate(ring_gather(mine, "x"), axis=0), "z").step(3)
    (own,) = ring.wait_for(own)
    sib = swap(own, ("core",), (1,))
    chunks = ring.finish()
    parts = lax.all_to_all(partial_half(own, sib, chunks), "y", 0, 0, tiled=True)
    half = parts.sum(axis=0).astype(BF16)

    z_blocks = ring_gather(half, "z")
    pair = jnp.stack([half, swap(half, ("x_lo",), (1,))])
    lines = [pair] + [lax.ppermute(pair, "y", [(i, (i - s) % NY) for i in range(NY)]) for s in (1, 2, 3)]
    xy_blocks = [lines[s][dx] for dx in range(2) for s in range(4)]

    other = tile_product(z_blocks, xy_blocks)
    mine = tile_product(z_blocks, xy_blocks, swap(other, ("core",), (1,)))
    pieces = lax.all_to_all(mine, ("x_hi", "x_lo", "y"), 0, 0, tiled=True)
    return assemble(pieces)


def solution(mesh):
    split = Mesh(mesh.devices.reshape(SIZES), AXES)
    row = ("z", "x_lo", "y")
    aux = ("x_hi", "core")
    return jax.shard_map(
        body,
        mesh=split,
        in_specs=(P(aux, row, None), P(row, None)),
        out_specs=P(row, aux),
        check_vma=False,
    )
```

```python
import jax
import jax.numpy as jnp
from jax import lax
from jax.experimental import pallas as pl
from jax.experimental.pallas import tpu as pltpu
from jax.sharding import Mesh
from jax.sharding import PartitionSpec as P

AXES = ("x_hi", "core", "z", "x_lo", "y")
SIZES = (2, 2, 8, 2, 4)
NZ, NX, NY = 8, 2, 4
ROWS = 128
N = 8192
OCC = 768
COLS = OCC // 2
F32 = jnp.float32
BF16 = jnp.bfloat16


def ring_pairs(size, step):
    pairs = []
    for core in range(2):
        sign = 1 - 2 * core
        for i in range(size):
            pairs.append((core * size + i, core * size + (i + sign * step) % size))
    return pairs


def ring_send(x, axis, step):
    size = SIZES[AXES.index(axis)]
    return lax.ppermute(x, ("core", axis), ring_pairs(size, step))


def x_send(x):
    pairs = []
    for core in range(2):
        for i in range(4):
            j = (i + 1 - 2 * core) % 4
            src = ((i // 2) * 2 + core) * 2 + i % 2
            dst = ((j // 2) * 2 + core) * 2 + j % 2
            pairs.append((src, dst))
    return lax.ppermute(x, ("x_hi", "core", "x_lo"), pairs)


def swap(x, axis):
    return lax.ppermute(x, axis, [(0, 1), (1, 0)])


def y_send(x, step):
    return lax.ppermute(x, "y", [(i, (i + step) % NY) for i in range(NY)])


Z_OFFSETS = (0, -1, 1, -2, 2, -3, 3, -4)


def z_gather(x, each_round=lambda blocks: ()):
    fwd, bwd = ring_send(x, "z", 1), ring_send(x, "z", -1)
    blocks, given = [x, fwd, bwd], [each_round([x, fwd, bwd])]
    fwd2, bwd2 = ring_send(fwd, "z", 1), ring_send(bwd, "z", -1)
    fwd2, bwd2, given[0] = lax.optimization_barrier((fwd2, bwd2, given[0]))
    given.append(each_round([fwd2, bwd2]))
    last = [ring_send(fwd2, "z", 1), ring_send(bwd2, "z", -1), ring_send(fwd2, "z", 2)]
    last, given[1] = lax.optimization_barrier((last, given[1]))
    given.append(each_round(last))
    return blocks + [fwd2, bwd2] + last, given


def z_slots():
    sign = 1 - 2 * lax.axis_index("core")
    return [(lax.axis_index("z") + sign * off) % NZ for off in Z_OFFSETS]


PARAMS = pltpu.CompilerParams(vmem_limit_bytes=12 << 20)


def by_y_kernel(x_ref, out_ref):
    for y in range(NY):
        for k in range(NZ * NX // NY):
            block = k * NY + y
            out_ref[y, :, k * ROWS : (k + 1) * ROWS] = x_ref[:, block * ROWS : (block + 1) * ROWS]


def columns_by_y(x):
    width = N // NY
    return pl.pallas_call(
        by_y_kernel,
        grid=(NY,),
        in_specs=[pl.BlockSpec((ROWS, width), lambda j: (0, j))],
        out_specs=pl.BlockSpec((NY, ROWS, width // NY), lambda j: (0, 0, j)),
        out_shape=jax.ShapeDtypeStruct((NY, ROWS, width), BF16),
    )(x)


def collect_kernel(*refs):
    near, far, out = refs[:8], refs[8:11], refs[11]
    x = lax.axis_index("x_lo")
    slots = z_slots()
    far_blocks = [(ref, k) for ref in far for k in range(ref.shape[0] // ROWS)]
    for k, z in enumerate(slots):
        here = pl.multiple_of((z * NX + x) * ROWS, ROWS)
        there = pl.multiple_of((z * NX + 1 - x) * ROWS, ROWS)
        out[pl.ds(here, ROWS)] = near[k][...]
        ref, i = far_blocks[k]
        out[pl.ds(there, ROWS)] = ref[i * ROWS : (i + 1) * ROWS]


def collect(near, far):
    return pl.pallas_call(
        collect_kernel, out_shape=jax.ShapeDtypeStruct((N // NY, COLS), BF16), compiler_params=PARAMS
    )(*near, *far)


def partial_kernel(steps, own_ref, sib_ref, rhs_ref, *outs):
    y = lax.axis_index("y")
    for step, out in zip(steps, outs):
        row = (y + step) % NY
        lhs = jnp.concatenate([own_ref[row], sib_ref[row]], axis=0)
        prod = jnp.dot(lhs, rhs_ref[...], preferred_element_type=F32)
        out[:, :COLS] = prod[:ROWS]
        out[:, COLS:] = prod[ROWS:]


def partial_half(own, sib, rhs, *steps):
    return pl.pallas_call(
        lambda *refs: partial_kernel(steps, *refs),
        out_shape=[jax.ShapeDtypeStruct((ROWS, OCC), F32)] * len(steps),
        compiler_params=PARAMS,
    )(own, sib, rhs)


def tile_kernel(keep, *refs):
    z_blocks, lines, refs = refs[:8], refs[8:12], refs[12:]
    added = refs[0] if keep else None
    out, z_buf, xy_buf = refs[-3:]
    core, x, y = lax.axis_index("core"), lax.axis_index("x_lo"), lax.axis_index("y")
    low = core if keep else 1 - core
    for k, z in enumerate(z_slots()):
        z_buf[z] = z_blocks[k][...]
    for s in range(NY):
        for dx in range(NX):
            xy_buf[((x + dx) % NX) * NY + (y + s) % NY] = lines[s][dx]
    for high in range(2):
        rhs = z_buf[pl.ds(4 * high + 2 * low, 2)].reshape(2 * ROWS, OCC)
        for k in range(0, 8, 4):
            prod = lax.dot_general(
                xy_buf[k : k + 4].reshape(4 * ROWS, OCC),
                rhs,
                (((1,), (1,)), ((), ())),
                preferred_element_type=F32,
            ).reshape(4, ROWS, 2 * ROWS)
            rows = slice(8 * high + k, 8 * high + k + 4)
            if keep:
                prod = prod + added[rows].astype(F32)
            out[rows] = prod.astype(BF16)


def tile_product(z_blocks, lines, *added):
    keep = bool(added)
    return pl.pallas_call(
        lambda *refs: tile_kernel(keep, *refs),
        out_shape=jax.ShapeDtypeStruct((16, ROWS, 2 * ROWS), BF16),
        scratch_shapes=[pltpu.VMEM((8, ROWS, OCC), BF16)] * 2,
        compiler_params=PARAMS,
    )(*z_blocks, *lines, *added)


def final_kernel(pieces, out):
    for k in range(4):
        out[:, k * ROWS : (k + 1) * ROWS] = pieces[0, k].astype(F32) + pieces[1, k].astype(F32)


def assemble(pieces):
    return pl.pallas_call(
        final_kernel,
        grid=(4,),
        in_specs=[pl.BlockSpec((2, 4, ROWS, ROWS), lambda j: (0, j % 2, 0, j // 2))],
        out_specs=pl.BlockSpec((ROWS, 4 * ROWS), lambda j: (0, j)),
        out_shape=jax.ShapeDtypeStruct((ROWS, 16 * ROWS), F32),
    )(pieces.reshape(2, 8, ROWS, 2 * ROWS))


def body(integrals, orbitals):
    own = lax.all_to_all(columns_by_y(integrals[0]), "y", 0, 0, tiled=True)
    core = lax.axis_index("core")
    mine = lax.dynamic_slice(orbitals, (0, core * COLS), (ROWS, COLS))
    near, far = z_gather(mine, lambda blocks: x_send(jnp.concatenate(blocks, axis=0)))
    own, far[-1] = lax.optimization_barrier((own, far[-1]))
    sib = swap(own, "core")
    rhs = collect(near, far)
    (across,) = partial_half(own, sib, rhs, 2)
    across = y_send(across, 2)
    up, down = partial_half(own, sib, rhs, 1, 3)
    up, down = y_send(up, 1), y_send(down, 3)
    (here,) = partial_half(own, sib, rhs, 0)
    half = (here + up + down + across).astype(BF16)

    pair = jnp.stack([half, swap(half, "x_lo")])
    lines = [pair] + [y_send(pair, -s) for s in (1, 2, 3)]
    z_blocks, _ = z_gather(half)

    other = tile_product(z_blocks, lines)
    mine = tile_product(z_blocks, lines, swap(other, "core"))
    pieces = lax.all_to_all(mine, ("x_hi", "x_lo", "y"), 0, 0, tiled=True)
    return assemble(pieces)


def solution(mesh):
    split = Mesh(mesh.devices.reshape(SIZES), AXES)
    row = ("z", "x_lo", "y")
    aux = ("x_hi", "core")
    return jax.shard_map(
        body,
        mesh=split,
        in_specs=(P(aux, row, None), P(row, None)),
        out_specs=P(row, aux),
        check_vma=False,
    )
```

```python
import jax
import jax.numpy as jnp
from jax import lax
from jax.experimental import pallas as pl
from jax.experimental.pallas import tpu as pltpu
from jax.sharding import Mesh
from jax.sharding import PartitionSpec as P

AXES = ("x_hi", "core", "z", "x_lo", "y")
SIZES = (2, 2, 8, 2, 4)
NZ, NX, NY = 8, 2, 4
ROWS = 128
N = 8192
OCC = 768
COLS = OCC // 2
F32 = jnp.float32
BF16 = jnp.bfloat16


def ring_pairs(size, step):
    pairs = []
    for core in range(2):
        sign = 1 - 2 * core
        for i in range(size):
            pairs.append((core * size + i, core * size + (i + sign * step) % size))
    return pairs


def ring_send(x, axis, step):
    size = SIZES[AXES.index(axis)]
    return lax.ppermute(x, ("core", axis), ring_pairs(size, step))


def x_send(x):
    pairs = []
    for core in range(2):
        for i in range(4):
            j = (i + 1 - 2 * core) % 4
            src = ((i // 2) * 2 + core) * 2 + i % 2
            dst = ((j // 2) * 2 + core) * 2 + j % 2
            pairs.append((src, dst))
    return lax.ppermute(x, ("x_hi", "core", "x_lo"), pairs)


def swap(x, axis):
    return lax.ppermute(x, axis, [(0, 1), (1, 0)])


def y_send(x, step):
    return lax.ppermute(x, "y", [(i, (i + step) % NY) for i in range(NY)])


Z_OFFSETS = (0, -1, 1, -2, 2, -3, 3, -4)


def z_gather(x, hops=1, in_step=False):
    blocks, fwd, bwd = [x], [x], [x]
    for k in range(3):
        if in_step and k:
            fwd[-1], bwd[-1] = lax.optimization_barrier((fwd[-1], bwd[-1]))
        fwd.append(ring_send(fwd[-1], "z", 1))
        bwd.append(ring_send(bwd[-1], "z", -1))
        blocks += [fwd[-1], bwd[-1]]
    return blocks + [ring_send(fwd[4 - hops], "z", hops)]


def z_slots():
    sign = 1 - 2 * lax.axis_index("core")
    return [(lax.axis_index("z") + sign * off) % NZ for off in Z_OFFSETS]


PARAMS = pltpu.CompilerParams(vmem_limit_bytes=12 << 20)


def by_y_kernel(x_ref, out_ref):
    for y in range(NY):
        for k in range(NZ * NX):
            block = k * NY + y
            out_ref[y, :, k * ROWS : (k + 1) * ROWS] = x_ref[:, block * ROWS : (block + 1) * ROWS]


def columns_by_y(x):
    return pl.pallas_call(
        by_y_kernel, out_shape=jax.ShapeDtypeStruct((NY, ROWS, N // NY), BF16), compiler_params=PARAMS
    )(x)


def collect_kernel(*refs):
    blocks, out = refs[:8], refs[8]
    x = lax.axis_index("x_lo")
    for k, z in enumerate(z_slots()):
        for dx in range(NX):
            slot = z * NX + (x + dx) % NX
            out[pl.ds(pl.multiple_of(slot * ROWS, ROWS), ROWS)] = blocks[k][dx * ROWS : (dx + 1) * ROWS]


def collect(blocks):
    return pl.pallas_call(
        collect_kernel, out_shape=jax.ShapeDtypeStruct((N // NY, COLS), BF16), compiler_params=PARAMS
    )(*blocks)


def partial_kernel(steps, own_ref, sib_ref, rhs_ref, *outs):
    y = lax.axis_index("y")
    for step, out in zip(steps, outs):
        row = (y + step) % NY
        lhs = jnp.concatenate([own_ref[row], sib_ref[row]], axis=0)
        prod = jnp.dot(lhs, rhs_ref[...], preferred_element_type=F32)
        out[:, :COLS] = prod[:ROWS]
        out[:, COLS:] = prod[ROWS:]


def partial_half(own, sib, rhs, *steps):
    return pl.pallas_call(
        lambda *refs: partial_kernel(steps, *refs),
        out_shape=[jax.ShapeDtypeStruct((ROWS, OCC), F32)] * len(steps),
        compiler_params=PARAMS,
    )(own, sib, rhs)


def tile_kernel(keep, *refs):
    z_blocks, lines, refs = refs[:8], refs[8:12], refs[12:]
    added = refs[0] if keep else None
    out, z_buf, xy_buf = refs[-3:]
    core, x, y = lax.axis_index("core"), lax.axis_index("x_lo"), lax.axis_index("y")
    low = core if keep else 1 - core
    for k, z in enumerate(z_slots()):
        z_buf[z] = z_blocks[k][...]
    for s in range(NY):
        for dx in range(NX):
            xy_buf[((x + dx) % NX) * NY + (y + s) % NY] = lines[s][dx]
    for high in range(2):
        rhs = z_buf[pl.ds(4 * high + 2 * low, 2)].reshape(2 * ROWS, OCC)
        for k in range(0, 8, 4):
            prod = lax.dot_general(
                xy_buf[k : k + 4].reshape(4 * ROWS, OCC),
                rhs,
                (((1,), (1,)), ((), ())),
                preferred_element_type=F32,
            ).reshape(4, ROWS, 2 * ROWS)
            rows = slice(8 * high + k, 8 * high + k + 4)
            if keep:
                prod = prod + added[rows].astype(F32)
            out[rows] = prod.astype(BF16)


def tile_product(z_blocks, lines, *added):
    keep = bool(added)
    return pl.pallas_call(
        lambda *refs: tile_kernel(keep, *refs),
        out_shape=jax.ShapeDtypeStruct((16, ROWS, 2 * ROWS), BF16),
        scratch_shapes=[pltpu.VMEM((8, ROWS, OCC), BF16)] * 2,
        compiler_params=PARAMS,
    )(*z_blocks, *lines, *added)


def final_kernel(pieces, out):
    for src in range(NX * NY):
        total = pieces[src].astype(F32) + pieces[NX * NY + src].astype(F32)
        for zl in range(2):
            start = (zl * NX * NY + src) * ROWS
            out[:, start : start + ROWS] = total[:, zl * ROWS : (zl + 1) * ROWS]


def assemble(pieces):
    return pl.pallas_call(
        final_kernel, out_shape=jax.ShapeDtypeStruct((ROWS, 16 * ROWS), F32), compiler_params=PARAMS
    )(pieces)


def body(integrals, orbitals):
    core = lax.axis_index("core")
    mine = lax.dynamic_slice(orbitals, (0, core * COLS), (ROWS, COLS))
    theirs, columns = lax.optimization_barrier((x_send(mine), columns_by_y(integrals[0])))
    own = lax.all_to_all(columns, "y", 0, 0, tiled=True)
    blocks = z_gather(jnp.concatenate([mine, theirs], axis=0), 2, True)
    own, blocks[5], blocks[6] = lax.optimization_barrier((own, blocks[5], blocks[6]))
    sib = swap(own, "core")
    rhs = collect(blocks)
    (across,) = partial_half(own, sib, rhs, 2)
    across = y_send(across, 2)
    up, down = partial_half(own, sib, rhs, 1, 3)
    up, down = y_send(up, 1), y_send(down, 3)
    (here,) = partial_half(own, sib, rhs, 0)
    half = (here + up + down + across).astype(BF16)

    pair = jnp.stack([half, swap(half, "x_lo")])
    lines = [pair] + [y_send(pair, -s) for s in (1, 2, 3)]
    z_blocks = z_gather(half)

    other = tile_product(z_blocks, lines)
    mine = tile_product(z_blocks, lines, swap(other, "core"))
    pieces = lax.all_to_all(mine, ("x_hi", "x_lo", "y"), 0, 0, tiled=True)
    return assemble(pieces)


def solution(mesh):
    split = Mesh(mesh.devices.reshape(SIZES), AXES)
    row = ("z", "x_lo", "y")
    aux = ("x_hi", "core")
    return jax.shard_map(
        body,
        mesh=split,
        in_specs=(P(aux, row, None), P(row, None)),
        out_specs=P(row, aux),
        check_vma=False,
    )
```

```python
import jax
import jax.numpy as jnp
from jax import lax
from jax.experimental import pallas as pl
from jax.experimental.pallas import tpu as pltpu
from jax.sharding import Mesh
from jax.sharding import PartitionSpec as P

AXES = ("x_hi", "core", "z", "x_lo", "y")
SIZES = (2, 2, 8, 2, 4)
NZ, NX, NY = 8, 2, 4
ROWS = 128
N = 8192
OCC = 768
COLS = OCC // 2
F32 = jnp.float32
BF16 = jnp.bfloat16


def ring_pairs(size, step):
    pairs = []
    for core in range(2):
        sign = 1 - 2 * core
        for i in range(size):
            pairs.append((core * size + i, core * size + (i + sign * step) % size))
    return pairs


def ring_send(x, axis, step):
    size = SIZES[AXES.index(axis)]
    return lax.ppermute(x, ("core", axis), ring_pairs(size, step))


def x_send(x):
    pairs = []
    for core in range(2):
        for i in range(4):
            j = (i + 1 - 2 * core) % 4
            src = ((i // 2) * 2 + core) * 2 + i % 2
            dst = ((j // 2) * 2 + core) * 2 + j % 2
            pairs.append((src, dst))
    return lax.ppermute(x, ("x_hi", "core", "x_lo"), pairs)


def swap(x, axis):
    return lax.ppermute(x, axis, [(0, 1), (1, 0)])


def y_send(x, step):
    return lax.ppermute(x, "y", [(i, (i + step) % NY) for i in range(NY)])


Z_OFFSETS = (0, -1, 1, -2, 2, -3, 3, -4)


def z_step(fwd, bwd):
    return ring_send(fwd, "z", 1), ring_send(bwd, "z", -1)


def z_gather(x):
    blocks, fwd, bwd = [x], x, x
    for _ in range(3):
        fwd, bwd = z_step(fwd, bwd)
        blocks += [fwd, bwd]
    return blocks + [ring_send(fwd, "z", 1)]


def z_slots():
    sign = 1 - 2 * lax.axis_index("core")
    return [(lax.axis_index("z") + sign * off) % NZ for off in Z_OFFSETS]


PARAMS = pltpu.CompilerParams(vmem_limit_bytes=12 << 20)


def by_y_kernel(x_ref, *outs):
    y = lax.axis_index("y")
    for s, out in enumerate(outs):
        for k in range(NZ * NX):
            start = pl.multiple_of((k * NY + (y + s) % NY) * ROWS, ROWS)
            out[:, k * ROWS : (k + 1) * ROWS] = x_ref[:, pl.ds(start, ROWS)]


def columns_by_y(x):
    shape = jax.ShapeDtypeStruct((ROWS, N // NY), BF16)
    return pl.pallas_call(by_y_kernel, out_shape=[shape] * NY, compiler_params=PARAMS)(x)


def collect_kernel(*refs):
    blocks, out = refs[:8], refs[8]
    x = lax.axis_index("x_lo")
    for k, z in enumerate(z_slots()):
        for dx in range(NX):
            slot = z * NX + (x + dx) % NX
            out[pl.ds(pl.multiple_of(slot * ROWS, ROWS), ROWS)] = blocks[k][dx * ROWS : (dx + 1) * ROWS]


def collect(blocks):
    return pl.pallas_call(
        collect_kernel, out_shape=jax.ShapeDtypeStruct((N // NY, COLS), BF16), compiler_params=PARAMS
    )(*blocks)


def partial_kernel(rhs_ref, *refs):
    count = len(refs) // 3
    for own, sib, out in zip(refs[:count], refs[count : 2 * count], refs[2 * count :]):
        lhs = jnp.concatenate([own[...], sib[...]], axis=0)
        prod = jnp.dot(lhs, rhs_ref[...], preferred_element_type=F32)
        out[:, :COLS] = prod[:ROWS]
        out[:, COLS:] = prod[ROWS:]


def partial_half(rhs, own, sib):
    return pl.pallas_call(
        partial_kernel,
        out_shape=[jax.ShapeDtypeStruct((ROWS, OCC), F32)] * len(own),
        compiler_params=PARAMS,
    )(rhs, *own, *sib)


def tile_kernel(keep, *refs):
    z_blocks, lines, refs = refs[:8], refs[8:12], refs[12:]
    added = refs[0] if keep else None
    out, z_buf, xy_buf = refs[-3:]
    core, x, y = lax.axis_index("core"), lax.axis_index("x_lo"), lax.axis_index("y")
    low = core if keep else 1 - core
    for k, z in enumerate(z_slots()):
        z_buf[z] = z_blocks[k][...]
    for s in range(NY):
        for dx in range(NX):
            xy_buf[((x + dx) % NX) * NY + (y + s) % NY] = lines[s][dx]
    for high in range(2):
        rhs = z_buf[pl.ds(4 * high + 2 * low, 2)].reshape(2 * ROWS, OCC)
        for k in range(0, 8, 4):
            prod = lax.dot_general(
                xy_buf[k : k + 4].reshape(4 * ROWS, OCC),
                rhs,
                (((1,), (1,)), ((), ())),
                preferred_element_type=F32,
            ).reshape(4, ROWS, 2 * ROWS)
            rows = slice(8 * high + k, 8 * high + k + 4)
            if keep:
                prod = prod + added[rows].astype(F32)
            out[rows] = prod.astype(BF16)


def tile_product(z_blocks, lines, *added):
    keep = bool(added)
    return pl.pallas_call(
        lambda *refs: tile_kernel(keep, *refs),
        out_shape=jax.ShapeDtypeStruct((16, ROWS, 2 * ROWS), BF16),
        scratch_shapes=[pltpu.VMEM((8, ROWS, OCC), BF16)] * 2,
        compiler_params=PARAMS,
    )(*z_blocks, *lines, *added)


def final_kernel(pieces, out):
    for src in range(NX * NY):
        total = pieces[src].astype(F32) + pieces[NX * NY + src].astype(F32)
        for zl in range(2):
            start = (zl * NX * NY + src) * ROWS
            out[:, start : start + ROWS] = total[:, zl * ROWS : (zl + 1) * ROWS]


def assemble(pieces):
    return pl.pallas_call(
        final_kernel, out_shape=jax.ShapeDtypeStruct((ROWS, 16 * ROWS), F32), compiler_params=PARAMS
    )(pieces)


def body(integrals, orbitals):
    core = lax.axis_index("core")
    mine = lax.dynamic_slice(orbitals, (0, core * COLS), (ROWS, COLS))
    theirs, columns = lax.optimization_barrier((x_send(mine), columns_by_y(integrals[0])))
    rows = [columns[0]] + [y_send(columns[s], s) for s in (1, 2, 3)]
    sib = [swap(rows[0], "core"), None, None, None]
    pair = jnp.concatenate([mine, theirs], axis=0)
    first = z_step(pair, pair)
    first, sib[0] = lax.optimization_barrier((first, sib[0]))
    second = z_step(*first)
    second, rows[1], rows[3] = lax.optimization_barrier((second, rows[1], rows[3]))
    third = z_step(*second)
    far = ring_send(second[0], "z", 2)
    sib[1], sib[3] = swap(rows[1], "core"), swap(rows[3], "core")
    third, far, rows[2] = lax.optimization_barrier((third, far, rows[2]))
    sib[2] = swap(rows[2], "core")
    rhs = collect([pair, *first, *second, *third, far])
    down, up = partial_half(rhs, [rows[1], rows[3]], [sib[1], sib[3]])
    down, up = y_send(down, -1), y_send(up, 1)
    (across,) = partial_half(rhs, [rows[2]], [sib[2]])
    across = y_send(across, 2)
    (here,) = partial_half(rhs, [rows[0]], [sib[0]])
    half = (here + up + down + across).astype(BF16)

    pair = jnp.stack([half, swap(half, "x_lo")])
    lines = [pair] + [y_send(pair, -s) for s in (1, 2, 3)]
    z_blocks = z_gather(half)

    other = tile_product(z_blocks, lines)
    mine = tile_product(z_blocks, lines, swap(other, "core"))
    pieces = lax.all_to_all(mine, ("x_hi", "x_lo", "y"), 0, 0, tiled=True)
    return assemble(pieces)


def solution(mesh):
    split = Mesh(mesh.devices.reshape(SIZES), AXES)
    row = ("z", "x_lo", "y")
    aux = ("x_hi", "core")
    return jax.shard_map(
        body,
        mesh=split,
        in_specs=(P(aux, row, None), P(row, None)),
        out_specs=P(row, aux),
        check_vma=False,
    )
```

```python
import jax
import jax.numpy as jnp
from jax import lax
from jax.experimental import pallas as pl
from jax.experimental.pallas import tpu as pltpu
from jax.sharding import Mesh
from jax.sharding import PartitionSpec as P

AXES = ("x_hi", "core", "z", "x_lo", "y")
SIZES = (2, 2, 8, 2, 4)
NZ, NX, NY = 8, 2, 4
ROWS = 128
N = 8192
OCC = 768
COLS = OCC // 2
F32 = jnp.float32
BF16 = jnp.bfloat16


def ring_pairs(size, step):
    pairs = []
    for core in range(2):
        sign = 1 - 2 * core
        for i in range(size):
            pairs.append((core * size + i, core * size + (i + sign * step) % size))
    return pairs


def ring_send(x, axis, step):
    size = SIZES[AXES.index(axis)]
    return lax.ppermute(x, ("core", axis), ring_pairs(size, step))


def x_send(x):
    pairs = []
    for core in range(2):
        for i in range(4):
            j = (i + 1 - 2 * core) % 4
            src = ((i // 2) * 2 + core) * 2 + i % 2
            dst = ((j // 2) * 2 + core) * 2 + j % 2
            pairs.append((src, dst))
    return lax.ppermute(x, ("x_hi", "core", "x_lo"), pairs)


def swap(x, axis):
    return lax.ppermute(x, axis, [(0, 1), (1, 0)])


def y_send(x, step):
    return lax.ppermute(x, "y", [(i, (i + step) % NY) for i in range(NY)])


Z_OFFSETS = (0, -1, 1, -2, 2, -3, 3, -4)


def z_step(fwd, bwd):
    return ring_send(fwd, "z", 1), ring_send(bwd, "z", -1)


def z_gather(x):
    first = z_step(x, x)
    second = z_step(*first)
    return [x, *first, *second, *z_step(*second), ring_send(second[0], "z", 2)]


def z_slots():
    sign = 1 - 2 * lax.axis_index("core")
    return [(lax.axis_index("z") + sign * off) % NZ for off in Z_OFFSETS]


PARAMS = pltpu.CompilerParams(vmem_limit_bytes=12 << 20)


def by_y_kernel(x_ref, *outs):
    y = lax.axis_index("y")
    for s, out in enumerate(outs):
        for k in range(NZ * NX):
            start = pl.multiple_of((k * NY + (y + s) % NY) * ROWS, ROWS)
            out[:, k * ROWS : (k + 1) * ROWS] = x_ref[:, pl.ds(start, ROWS)]


def columns_by_y(x):
    shape = jax.ShapeDtypeStruct((ROWS, N // NY), BF16)
    return pl.pallas_call(by_y_kernel, out_shape=[shape] * NY, compiler_params=PARAMS)(x)


def collect_kernel(*refs):
    blocks, out = refs[:8], refs[8]
    x = lax.axis_index("x_lo")
    for k, z in enumerate(z_slots()):
        for dx in range(NX):
            slot = z * NX + (x + dx) % NX
            out[pl.ds(pl.multiple_of(slot * ROWS, ROWS), ROWS)] = blocks[k][dx * ROWS : (dx + 1) * ROWS]


def collect(blocks):
    return pl.pallas_call(
        collect_kernel, out_shape=jax.ShapeDtypeStruct((N // NY, COLS), BF16), compiler_params=PARAMS
    )(*blocks)


def partial_kernel(rhs_ref, *refs):
    count = len(refs) // 3
    for own, sib, out in zip(refs[:count], refs[count : 2 * count], refs[2 * count :]):
        lhs = jnp.concatenate([own[...], sib[...]], axis=0)
        prod = jnp.dot(lhs, rhs_ref[...], preferred_element_type=F32)
        out[:, :COLS] = prod[:ROWS]
        out[:, COLS:] = prod[ROWS:]


def partial_half(rhs, own, sib):
    return pl.pallas_call(
        partial_kernel,
        out_shape=[jax.ShapeDtypeStruct((ROWS, OCC), F32)] * len(own),
        compiler_params=PARAMS,
    )(rhs, *own, *sib)


def tile_kernel(keep, *refs):
    z_blocks, lines, refs = refs[:8], refs[8:12], refs[12:]
    added = refs[0] if keep else None
    out, z_buf, xy_buf = refs[-3:]
    core, x, y = lax.axis_index("core"), lax.axis_index("x_lo"), lax.axis_index("y")
    low = core if keep else 1 - core
    for k, z in enumerate(z_slots()):
        z_buf[z] = z_blocks[k][...]
    for s in range(NY):
        for dx in range(NX):
            xy_buf[((x + dx) % NX) * NY + (y + s) % NY] = lines[s][dx]
    for high in range(2):
        rhs = z_buf[pl.ds(4 * high + 2 * low, 2)].reshape(2 * ROWS, OCC)
        for k in range(0, 8, 4):
            prod = lax.dot_general(
                xy_buf[k : k + 4].reshape(4 * ROWS, OCC),
                rhs,
                (((1,), (1,)), ((), ())),
                preferred_element_type=F32,
            ).reshape(4, ROWS, 2 * ROWS)
            rows = slice(8 * high + k, 8 * high + k + 4)
            if keep:
                prod = prod + added[rows].astype(F32)
            out[rows] = prod.astype(BF16)


def tile_product(z_blocks, lines, *added):
    keep = bool(added)
    return pl.pallas_call(
        lambda *refs: tile_kernel(keep, *refs),
        out_shape=jax.ShapeDtypeStruct((16, ROWS, 2 * ROWS), BF16),
        scratch_shapes=[pltpu.VMEM((8, ROWS, OCC), BF16)] * 2,
        compiler_params=PARAMS,
    )(*z_blocks, *lines, *added)


def final_kernel(pieces, out):
    for src in range(NX * NY):
        total = pieces[src].astype(F32) + pieces[NX * NY + src].astype(F32)
        for zl in range(2):
            start = (zl * NX * NY + src) * ROWS
            out[:, start : start + ROWS] = total[:, zl * ROWS : (zl + 1) * ROWS]


def assemble(pieces):
    return pl.pallas_call(
        final_kernel, out_shape=jax.ShapeDtypeStruct((ROWS, 16 * ROWS), F32), compiler_params=PARAMS
    )(pieces)


def body(integrals, orbitals):
    core = lax.axis_index("core")
    mine = lax.dynamic_slice(orbitals, (0, core * COLS), (ROWS, COLS))
    theirs, columns = lax.optimization_barrier((x_send(mine), columns_by_y(integrals[0])))
    rows = [columns[0]] + [y_send(columns[s], s) for s in (1, 2, 3)]
    sib = [swap(rows[0], "core"), None, None, None]
    pair = jnp.concatenate([mine, theirs], axis=0)
    first = z_step(pair, pair)
    first, sib[0] = lax.optimization_barrier((first, sib[0]))
    fwd, bwd = z_step(*first)
    bwd, rows[1], rows[3] = lax.optimization_barrier((bwd, rows[1], rows[3]))
    second = [fwd, bwd]
    third = z_step(*second)
    far = ring_send(fwd, "z", 2)
    sib[1], sib[3] = swap(rows[1], "core"), swap(rows[3], "core")
    third, far, rows[2] = lax.optimization_barrier((third, far, rows[2]))
    sib[2] = swap(rows[2], "core")
    rhs = collect([pair, *first, *second, *third, far])
    (across,) = partial_half(rhs, [rows[2]], [sib[2]])
    rhs, across = lax.optimization_barrier((rhs, across))
    across = y_send(across, 2)
    down, up = partial_half(rhs, [rows[1], rows[3]], [sib[1], sib[3]])
    down, up = y_send(down, -1), y_send(up, 1)
    (here,) = partial_half(rhs, [rows[0]], [sib[0]])
    half = (here + up + down + across).astype(BF16)

    pair = jnp.stack([half, swap(half, "x_lo")])
    far = y_send(half, -2)
    lines = [pair, y_send(pair, -1), jnp.stack([far, swap(far, "x_lo")]), y_send(pair, -3)]
    z_blocks = z_gather(half)

    other = tile_product(z_blocks, lines)
    mine = tile_product(z_blocks, lines, swap(other, "core"))
    pieces = lax.all_to_all(mine, ("x_hi", "x_lo", "y"), 0, 0, tiled=True)
    return assemble(pieces)


def solution(mesh):
    split = Mesh(mesh.devices.reshape(SIZES), AXES)
    row = ("z", "x_lo", "y")
    aux = ("x_hi", "core")
    return jax.shard_map(
        body,
        mesh=split,
        in_specs=(P(aux, row, None), P(row, None)),
        out_specs=P(row, aux),
        check_vma=False,
    )
```

```python
import jax
import jax.numpy as jnp
from jax import lax
from jax.experimental import pallas as pl
from jax.experimental.pallas import tpu as pltpu
from jax.sharding import Mesh
from jax.sharding import PartitionSpec as P

AXES = ("x_hi", "core", "z", "x_lo", "y")
SIZES = (2, 2, 8, 2, 4)
NZ, NX, NY = 8, 2, 4
ROWS = 128
N = 8192
OCC = 768
COLS = OCC // 2
F32 = jnp.float32
BF16 = jnp.bfloat16


def ring_pairs(size, step):
    pairs = []
    for core in range(2):
        sign = 1 - 2 * core
        for i in range(size):
            pairs.append((core * size + i, core * size + (i + sign * step) % size))
    return pairs


def ring_send(x, axis, step):
    size = SIZES[AXES.index(axis)]
    return lax.ppermute(x, ("core", axis), ring_pairs(size, step))


def x_send(x):
    pairs = []
    for core in range(2):
        for i in range(4):
            j = (i + 1 - 2 * core) % 4
            src = ((i // 2) * 2 + core) * 2 + i % 2
            dst = ((j // 2) * 2 + core) * 2 + j % 2
            pairs.append((src, dst))
    return lax.ppermute(x, ("x_hi", "core", "x_lo"), pairs)


def swap(x, axis):
    return lax.ppermute(x, axis, [(0, 1), (1, 0)])


def y_send(x, step):
    return lax.ppermute(x, "y", [(i, (i + step) % NY) for i in range(NY)])


Z_OFFSETS = (0, -1, 1, -2, 2, -3, 3, -4)


def z_step(fwd, bwd):
    return ring_send(fwd, "z", 1), ring_send(bwd, "z", -1)


def z_gather(x):
    first = z_step(x, x)
    second = z_step(*first)
    return [x, *first, *second, *z_step(*second), ring_send(second[0], "z", 2)]


def z_slots():
    sign = 1 - 2 * lax.axis_index("core")
    return [(lax.axis_index("z") + sign * off) % NZ for off in Z_OFFSETS]


PARAMS = pltpu.CompilerParams(vmem_limit_bytes=12 << 20)


def by_y_kernel(x_ref, *outs):
    y = lax.axis_index("y")
    for s, out in enumerate(outs):
        for k in range(NZ * NX):
            start = pl.multiple_of((k * NY + (y + s) % NY) * ROWS, ROWS)
            out[:, k * ROWS : (k + 1) * ROWS] = x_ref[:, pl.ds(start, ROWS)]


def columns_by_y(x):
    shape = jax.ShapeDtypeStruct((ROWS, N // NY), BF16)
    return pl.pallas_call(by_y_kernel, out_shape=[shape] * NY, compiler_params=PARAMS)(x)


def collect_kernel(*refs):
    blocks, out = refs[:8], refs[8]
    x = lax.axis_index("x_lo")
    for k, z in enumerate(z_slots()):
        for dx in range(NX):
            slot = z * NX + (x + dx) % NX
            out[pl.ds(pl.multiple_of(slot * ROWS, ROWS), ROWS)] = blocks[k][dx * ROWS : (dx + 1) * ROWS]


def collect(blocks):
    return pl.pallas_call(
        collect_kernel, out_shape=jax.ShapeDtypeStruct((N // NY, COLS), BF16), compiler_params=PARAMS
    )(*blocks)


def partial_kernel(rhs_ref, *refs):
    count = len(refs) // 3
    for own, sib, out in zip(refs[:count], refs[count : 2 * count], refs[2 * count :]):
        lhs = jnp.concatenate([own[...], sib[...]], axis=0)
        prod = jnp.dot(lhs, rhs_ref[...], preferred_element_type=F32)
        out[:, :COLS] = prod[:ROWS]
        out[:, COLS:] = prod[ROWS:]


def partial_half(rhs, own, sib):
    return pl.pallas_call(
        partial_kernel,
        out_shape=[jax.ShapeDtypeStruct((ROWS, OCC), F32)] * len(own),
        compiler_params=PARAMS,
    )(rhs, *own, *sib)


def tile_kernel(keep, *refs):
    z_blocks, lines, refs = refs[:8], refs[8:12], refs[12:]
    added = refs[0] if keep else None
    out, z_buf, xy_buf = refs[-3:]
    core, x, y = lax.axis_index("core"), lax.axis_index("x_lo"), lax.axis_index("y")
    low = core if keep else 1 - core
    for k, z in enumerate(z_slots()):
        z_buf[z] = z_blocks[k][...]
    for s in range(NY):
        for dx in range(NX):
            xy_buf[((x + dx) % NX) * NY + (y + s) % NY] = lines[s][dx]
    for high in range(2):
        rhs = z_buf[pl.ds(4 * high + 2 * low, 2)].reshape(2 * ROWS, OCC)
        for k in range(0, 8, 4):
            prod = lax.dot_general(
                xy_buf[k : k + 4].reshape(4 * ROWS, OCC),
                rhs,
                (((1,), (1,)), ((), ())),
                preferred_element_type=F32,
            ).reshape(4, ROWS, 2 * ROWS)
            rows = slice(8 * high + k, 8 * high + k + 4)
            if keep:
                prod = prod + added[rows].astype(F32)
            out[rows] = prod.astype(BF16)


def tile_product(z_blocks, lines, *added):
    keep = bool(added)
    return pl.pallas_call(
        lambda *refs: tile_kernel(keep, *refs),
        out_shape=jax.ShapeDtypeStruct((16, ROWS, 2 * ROWS), BF16),
        scratch_shapes=[pltpu.VMEM((8, ROWS, OCC), BF16)] * 2,
        compiler_params=PARAMS,
    )(*z_blocks, *lines, *added)


def final_kernel(pieces, out):
    for src in range(NX * NY):
        total = pieces[src].astype(F32) + pieces[NX * NY + src].astype(F32)
        for zl in range(2):
            start = (zl * NX * NY + src) * ROWS
            out[:, start : start + ROWS] = total[:, zl * ROWS : (zl + 1) * ROWS]


def assemble(pieces):
    return pl.pallas_call(
        final_kernel, out_shape=jax.ShapeDtypeStruct((ROWS, 16 * ROWS), F32), compiler_params=PARAMS
    )(pieces)


def body(integrals, orbitals):
    core = lax.axis_index("core")
    mine = lax.dynamic_slice(orbitals, (0, core * COLS), (ROWS, COLS))
    theirs, columns = lax.optimization_barrier((x_send(mine), columns_by_y(integrals[0])))
    rows = [columns[0]] + [y_send(columns[s], s) for s in (1, 2, 3)]
    sib = [swap(rows[0], "core"), None, None, None]
    pair = jnp.concatenate([mine, theirs], axis=0)
    first = z_step(pair, pair)
    first = lax.optimization_barrier(first)
    fwd, bwd = z_step(*first)
    bwd, rows[1], rows[3] = lax.optimization_barrier((bwd, rows[1], rows[3]))
    second = [fwd, bwd]
    third = z_step(*second)
    far = ring_send(fwd, "z", 2)
    sib[1], sib[3] = swap(rows[1], "core"), swap(rows[3], "core")
    third, far, rows[2] = lax.optimization_barrier((third, far, rows[2]))
    sib[2] = swap(rows[2], "core")
    rhs = collect([pair, *first, *second, *third, far])
    down, up = partial_half(rhs, [rows[1], rows[3]], [sib[1], sib[3]])
    down, up = y_send(down, -1), y_send(up, 1)
    (across,) = partial_half(rhs, [rows[2]], [sib[2]])
    across = y_send(across, 2)
    (here,) = partial_half(rhs, [rows[0]], [sib[0]])
    half = (here + up + down + across).astype(BF16)

    pair = jnp.stack([half, swap(half, "x_lo")])
    far = y_send(half, -2)
    lines = [pair, y_send(pair, -1), jnp.stack([far, swap(far, "x_lo")]), y_send(pair, -3)]
    z_blocks = z_gather(half)

    other = tile_product(z_blocks, lines)
    mine = tile_product(z_blocks, lines, swap(other, "core"))
    pieces = lax.all_to_all(mine, ("x_hi", "x_lo", "y"), 0, 0, tiled=True)
    return assemble(pieces)


def solution(mesh):
    split = Mesh(mesh.devices.reshape(SIZES), AXES)
    row = ("z", "x_lo", "y")
    aux = ("x_hi", "core")
    return jax.shard_map(
        body,
        mesh=split,
        in_specs=(P(aux, row, None), P(row, None)),
        out_specs=P(row, aux),
        check_vma=False,
    )
```

```python
import jax
import jax.numpy as jnp
from jax import lax
from jax.experimental import pallas as pl
from jax.experimental.pallas import tpu as pltpu
from jax.sharding import Mesh
from jax.sharding import PartitionSpec as P

AXES = ("x_hi", "core", "z", "x_lo", "y")
SIZES = (2, 2, 8, 2, 4)
NZ, NX, NY = 8, 2, 4
ROWS = 128
N = 8192
OCC = 768
COLS = OCC // 2
F32 = jnp.float32
BF16 = jnp.bfloat16


def ring_pairs(size, step):
    pairs = []
    for core in range(2):
        sign = 1 - 2 * core
        for i in range(size):
            pairs.append((core * size + i, core * size + (i + sign * step) % size))
    return pairs


def ring_send(x, axis, step):
    size = SIZES[AXES.index(axis)]
    return lax.ppermute(x, ("core", axis), ring_pairs(size, step))


def x_send(x):
    pairs = []
    for core in range(2):
        for i in range(4):
            j = (i + 1 - 2 * core) % 4
            src = ((i // 2) * 2 + core) * 2 + i % 2
            dst = ((j // 2) * 2 + core) * 2 + j % 2
            pairs.append((src, dst))
    return lax.ppermute(x, ("x_hi", "core", "x_lo"), pairs)


def swap(x, axis):
    return lax.ppermute(x, axis, [(0, 1), (1, 0)])


def y_send(x, step):
    return lax.ppermute(x, "y", [(i, (i + step) % NY) for i in range(NY)])


Z_OFFSETS = (0, -1, 1, -2, 2, -3, 3, -4)


def z_step(fwd, bwd):
    return ring_send(fwd, "z", 1), ring_send(bwd, "z", -1)


def z_gather(x):
    first = z_step(x, x)
    second = z_step(*first)
    return [x, *first, *second, *z_step(*second), ring_send(second[0], "z", 2)]


def z_slots():
    sign = 1 - 2 * lax.axis_index("core")
    return [(lax.axis_index("z") + sign * off) % NZ for off in Z_OFFSETS]


PARAMS = pltpu.CompilerParams(vmem_limit_bytes=12 << 20)


def by_y_kernel(x_ref, *outs):
    y = lax.axis_index("y")
    for s, out in enumerate(outs):
        for k in range(NZ * NX):
            start = pl.multiple_of((k * NY + (y + s) % NY) * ROWS, ROWS)
            out[:, k * ROWS : (k + 1) * ROWS] = x_ref[:, pl.ds(start, ROWS)]


def columns_by_y(x):
    shape = jax.ShapeDtypeStruct((ROWS, N // NY), BF16)
    return pl.pallas_call(by_y_kernel, out_shape=[shape] * NY, compiler_params=PARAMS)(x)


def collect_kernel(*refs):
    blocks, out = refs[:8], refs[8]
    x = lax.axis_index("x_lo")
    for k, z in enumerate(z_slots()):
        for dx in range(NX):
            slot = z * NX + (x + dx) % NX
            out[pl.ds(pl.multiple_of(slot * ROWS, ROWS), ROWS)] = blocks[k][dx * ROWS : (dx + 1) * ROWS]


def collect(blocks):
    return pl.pallas_call(
        collect_kernel, out_shape=jax.ShapeDtypeStruct((N // NY, COLS), BF16), compiler_params=PARAMS
    )(*blocks)


def partial_kernel(rhs_ref, *refs):
    count = len(refs) // 3
    for own, sib, out in zip(refs[:count], refs[count : 2 * count], refs[2 * count :]):
        lhs = jnp.concatenate([own[...], sib[...]], axis=0)
        prod = jnp.dot(lhs, rhs_ref[...], preferred_element_type=F32)
        out[:, :COLS] = prod[:ROWS]
        out[:, COLS:] = prod[ROWS:]


def partial_half(rhs, own, sib):
    return pl.pallas_call(
        partial_kernel,
        out_shape=[jax.ShapeDtypeStruct((ROWS, OCC), F32)] * len(own),
        compiler_params=PARAMS,
    )(rhs, *own, *sib)


def tile_kernel(keep, *refs):
    z_blocks, lines, refs = refs[:8], refs[8:12], refs[12:]
    out, z_buf, xy_buf = refs[-3:]
    core, x, y = lax.axis_index("core"), lax.axis_index("x_lo"), lax.axis_index("y")
    low = core if keep else 1 - core
    for k, z in enumerate(z_slots()):
        z_buf[z] = z_blocks[k][...]
    for s in range(NY):
        for dx in range(NX):
            xy_buf[((x + dx) % NX) * NY + (y + s) % NY] = lines[s][dx]
    for high in range(2):
        rhs = z_buf[pl.ds(4 * high + 2 * low, 2)].reshape(2 * ROWS, OCC)
        for k in range(0, 8, 4):
            prod = lax.dot_general(
                xy_buf[k : k + 4].reshape(4 * ROWS, OCC),
                rhs,
                (((1,), (1,)), ((), ())),
                preferred_element_type=F32,
            ).reshape(4, ROWS, 2 * ROWS)
            rows = slice(8 * high + k, 8 * high + k + 4)
            out[rows] = prod.astype(out.dtype)


def tile_product(z_blocks, lines, keep):
    return pl.pallas_call(
        lambda *refs: tile_kernel(keep, *refs),
        out_shape=jax.ShapeDtypeStruct((16, ROWS, 2 * ROWS), F32 if keep else BF16),
        scratch_shapes=[pltpu.VMEM((8, ROWS, OCC), BF16)] * 2,
        compiler_params=PARAMS,
    )(*z_blocks, *lines)


def final_kernel(pieces, out):
    for src in range(NX * NY):
        total = pieces[src].astype(F32) + pieces[NX * NY + src].astype(F32)
        for zl in range(2):
            start = (zl * NX * NY + src) * ROWS
            out[:, start : start + ROWS] = total[:, zl * ROWS : (zl + 1) * ROWS]


def assemble(pieces):
    return pl.pallas_call(
        final_kernel, out_shape=jax.ShapeDtypeStruct((ROWS, 16 * ROWS), F32), compiler_params=PARAMS
    )(pieces)


def body(integrals, orbitals):
    core = lax.axis_index("core")
    mine = lax.dynamic_slice(orbitals, (0, core * COLS), (ROWS, COLS))
    theirs, columns = lax.optimization_barrier((x_send(mine), columns_by_y(integrals[0])))
    rows = [columns[0]] + [y_send(columns[s], s) for s in (1, 2, 3)]
    sib = [swap(rows[0], "core"), None, None, None]
    pair = jnp.concatenate([mine, theirs], axis=0)
    first = z_step(pair, pair)
    first = lax.optimization_barrier(first)
    fwd, bwd = z_step(*first)
    bwd, rows[1], rows[3] = lax.optimization_barrier((bwd, rows[1], rows[3]))
    second = [fwd, bwd]
    third = z_step(*second)
    far = ring_send(fwd, "z", 2)
    sib[1], sib[3] = swap(rows[1], "core"), swap(rows[3], "core")
    third, far, rows[2] = lax.optimization_barrier((third, far, rows[2]))
    sib[2] = swap(rows[2], "core")
    rhs = collect([pair, *first, *second, *third, far])
    down, up = partial_half(rhs, [rows[1], rows[3]], [sib[1], sib[3]])
    down, up = y_send(down, -1), y_send(up, 1)
    (across,) = partial_half(rhs, [rows[2]], [sib[2]])
    across = y_send(across, 2)
    (here,) = partial_half(rhs, [rows[0]], [sib[0]])
    half = (here + up + down + across).astype(BF16)

    pair = jnp.stack([half, swap(half, "x_lo")])
    far = y_send(half, -2)
    lines = [pair, y_send(pair, -1), jnp.stack([far, swap(far, "x_lo")]), y_send(pair, -3)]
    z_blocks = z_gather(half)

    arriving = swap(tile_product(z_blocks, lines, False), "core")
    mine = tile_product(z_blocks, lines, True)
    mine = (mine + arriving.astype(F32)).astype(BF16)
    pieces = lax.all_to_all(mine, ("x_hi", "x_lo", "y"), 0, 0, tiled=True)
    return assemble(pieces)


def solution(mesh):
    split = Mesh(mesh.devices.reshape(SIZES), AXES)
    row = ("z", "x_lo", "y")
    aux = ("x_hi", "core")
    return jax.shard_map(
        body,
        mesh=split,
        in_specs=(P(aux, row, None), P(row, None)),
        out_specs=P(row, aux),
        check_vma=False,
    )
```
